32 devices in a mesh: groups: 2 (over y), seq: 4 (over z), ep: 2 (over x), tp: 2 (over core).
Axes of the slice: x: 2, y: 2, z: 4, core: 2. Of those that a mesh axis runs over, the one named last changes fastest.
Arguments:
- hidden: bfloat16 [2048, 1440], P(('groups', 'seq', 'ep')), parts along dimension 0, may hold values from -6 to 6
- expert_ids: int32 [2048, 4], P(('groups', 'seq', 'ep')), parts along dimension 0, may hold values from 0 to 7, all different within a row; in each aligned block of 128 rows (0 to 127, 128 to 255, ...) at most 88 rows name the same one
- gate_units: int32 [2048, 4], P(('groups', 'seq', 'ep')), parts along dimension 0, may hold values from 4096 to 32767
- w_gate: bfloat16 [8, 1440, 1440], P(('seq', 'tp'), None, 'ep'), may hold values from -0.15625 to 0.15625
- w_up: bfloat16 [8, 1440, 1440], P(('seq', 'tp'), None, 'ep'), may hold values from -0.15625 to 0.15625
- w_down: bfloat16 [8, 1440, 1440], P(('seq', 'tp'), None, 'ep'), may hold values from -0.15625 to 0.15625
Outputs:
- moe_out: bfloat16 [2048, 1440], P(('groups', 'seq', 'ep'), 'tp'), parts along dimension 0
The draws below stay inside these ranges and needn't reach their ends.
There are 2 independent parts, one for each index of `groups`. The reference program is written for one: setup_inputs(seed, part) draws one part's arguments, and reference() takes and returns one part's arrays. A program takes and returns all parts, laid end to end along the dimension named above; an argument that names none is the same for every part. Nothing has to cross between parts.
Inputs may be any that keep to these rules, and one draw needn't show every extreme that they name: `expert_ids`: each row names 4 different experts; in each aligned block of 128 rows no expert is named by more than 88 rows, and in every draw some expert is named by exactly 88 rows of some block.
All inputs are finite; a program needn't handle non-finite values.
Results may differ from the reference program's by a relative error of at most 0.0064.
Values may be sent and summed in bfloat16 or wider, within the bound.
A program may use at most 64 MiB of HBM per device.

```python
import math
import jax
import jax.numpy as jnp
import numpy as np
from jax import lax

D = 1440
FF = 1440
TOP = 4
TOK_DEV = 128
DOCUMENT_TOKENS = 1024
EXPERTS = 8
CAP = 88
N_EP = 2


def plant(result, key, least, largest):
    longest = result.shape.index(max(result.shape))
    spots = []
    for shift in (0, 1):
        where = [jax.random.randint(jax.random.fold_in(key, axis), (), 0, length) for axis, length in enumerate(result.shape)]
        where[longest] = (where[longest] + shift) % result.shape[longest]
        spots.append(tuple(where))
    return result.at[spots[0]].set(least).at[spots[1]].set(largest)


def levels(key, shape, shards, smallest, top_value):
    loudness = 1.0
    for position, shards_of in shards:
        draws = jax.random.uniform(jax.random.fold_in(jax.random.fold_in(key, 6), position), (shards_of,), jnp.float32, smallest / len(shards), top_value / len(shards))
        loudness = loudness * jnp.repeat(jnp.exp(draws), shape[position] // shards_of).reshape((-1,) + (1,) * (len(shape) - 1 - position))
    return loudness


def assign_block(key, own, number, rows, amount, top, limit, slope):
    order = jax.random.permutation(key, amount)
    crowded, ordinary = load_shares(amount, rows * top, limit, slope, True), load_shares(amount, rows * top, limit, slope, False)
    places = jnp.arange(amount)

    def named(sizes, rotation):
        used = int((sizes > 0).sum())
        fixed = max(1, used // 4)
        shifted = fixed + (places - fixed + rotation * (used - fixed)) % max(1, amount - fixed)
        return jnp.zeros((amount,), jnp.int32).at[order[jnp.where(places < fixed, places, shifted)]].set(jnp.asarray(sizes, jnp.int32))

    sizes = jnp.where(number % 4 == 0, named(crowded, number // 4), named(ordinary, number - number // 4 - 1))
    mixed = jax.random.permutation(jax.random.fold_in(own, 3), amount)
    giver, taker = mixed[0:amount // 2 * 2:2], mixed[1:amount // 2 * 2:2]
    room = jnp.minimum(sizes[giver] - 1, limit - sizes[taker]) // 2
    room = jnp.where((giver == order[0]) | (taker == order[0]) | (sizes[taker] == 0), 0, jnp.maximum(room, 0))
    shifted = jax.random.randint(jax.random.fold_in(own, 4), (amount // 2,), 0, 1 << 20) % (room + 1)
    sizes = sizes.at[giver].add(-shifted).at[taker].add(shifted)
    items = jnp.searchsorted(jnp.cumsum(sizes), jnp.arange(rows * top), side="right").astype(jnp.int32)
    listing = items.reshape(top, rows).T
    listing = listing[jax.random.permutation(jax.random.fold_in(own, 1), rows)]
    rotation = jax.random.randint(jax.random.fold_in(own, 2), (rows, 1), 0, top)
    return jnp.take_along_axis(listing, (jnp.arange(top)[None, :] + rotation) % top, axis=1)


def load_shares(amount, total, most, lean, full):
    portions = [(1 << 20) // math.isqrt(rank ** lean) + 1 for rank in range(1, amount + 1)]
    largest = most if full else min(most, max(-(-total // amount), total * portions[0] // sum(portions)))
    least = 1 if total - largest >= amount - 1 else 0
    counts, surplus = [largest] + [least] * (amount - 1), total - largest - least * (amount - 1)
    while surplus > 0:
        movable = [i for i in range(1, amount) if counts[i] < largest] or [i for i in range(1, amount) if counts[i] < most]
        whole, left = sum([portions[i] for i in movable]), surplus
        for i in movable:
            extra = min(most - counts[i], max(1, left * portions[i] // whole), surplus)
            counts[i] = counts[i] + extra
            surplus = surplus - extra
    return np.array(counts)


def bell_draw(stream_key, dims, scale, limit, cuts=(), kind=jnp.bfloat16):
    drawn = jax.random.normal(stream_key, dims, jnp.float32) * scale
    if len(cuts) > 0:
        drawn = levels(stream_key, dims, cuts, -0.22, 0.18) * drawn
    return jnp.clip(drawn, min=-limit, max=limit).astype(kind)


def setup_inputs(seed: int = 0, part: int = 0) -> dict:
    keys = jax.random.split(jax.random.key(seed), 7)
    part_keys = jax.random.split(jax.random.fold_in(keys[6], part), 7)
    hidden = bell_draw(part_keys[0], (DOCUMENT_TOKENS, D), 1.0, 6.0, ((0, 8),))
    expert_ids_keys = jax.random.split(jax.random.fold_in(part_keys[1], 1), DOCUMENT_TOKENS // TOK_DEV)
    expert_ids_turns = jax.random.permutation(jax.random.fold_in(part_keys[1], 3), DOCUMENT_TOKENS // TOK_DEV)
    expert_ids = jax.vmap(lambda own, number: assign_block(jax.random.fold_in(part_keys[1], 2), own, number, TOK_DEV, EXPERTS, TOP, CAP, 2))(expert_ids_keys, expert_ids_turns).reshape((DOCUMENT_TOKENS, TOP))
    gate_units = plant(jax.random.randint(part_keys[2], (DOCUMENT_TOKENS, TOP), 4096, 32768), jax.random.fold_in(part_keys[2], 1), 4096, 32767).astype(jnp.int32)
    w_gate = bell_draw(keys[3], (EXPERTS, D, FF), D ** -0.5, 0.15625, ((0, 8), (2, 2)))
    w_up = bell_draw(keys[4], (EXPERTS, D, FF), D ** -0.5, 0.15625, ((0, 8), (2, 2)))
    w_down = bell_draw(keys[5], (EXPERTS, D, FF), FF ** -0.5, 0.15625, ((0, 8), (2, 2)))
    return dict(hidden=hidden, expert_ids=expert_ids, gate_units=gate_units, w_gate=w_gate, w_up=w_up, w_down=w_down)


def expert_part(hidden, expert_ids, gate_units, w_gate, w_up, w_down):
    block_count = DOCUMENT_TOKENS // TOK_DEV
    pair_ids = expert_ids.reshape(block_count, TOK_DEV * TOP)
    onehot_ids = (pair_ids[:, :, None] == jnp.arange(EXPERTS, dtype=jnp.int32)[None, None, :]).astype(jnp.int32)
    slot_rank = jnp.sum((jnp.cumsum(onehot_ids, axis=1) - 1) * onehot_ids, axis=2).astype(jnp.int32)
    pair_index = jnp.arange(DOCUMENT_TOKENS * TOP, dtype=jnp.int32).reshape(block_count, TOK_DEV * TOP)
    block_index = jnp.broadcast_to(jnp.arange(block_count, dtype=jnp.int32)[:, None], pair_ids.shape)
    table = jnp.full((EXPERTS, block_count, CAP), -1, jnp.int32).at[pair_ids, block_index, slot_rank].set(pair_index)
    gate_share = gate_units.reshape(-1).astype(jnp.float32) / 65536.0
    slice_width = FF // N_EP

    def one_expert(running, expert):
        slots = table[expert].reshape(-1)
        live = slots >= 0
        safe = jnp.where(live, slots, 0).astype(jnp.int32)
        token_at = (safe // TOP).astype(jnp.int32)
        rows_in = hidden[token_at]
        gate_all = lax.dynamic_index_in_dim(w_gate, expert, 0, keepdims=False)
        up_all = lax.dynamic_index_in_dim(w_up, expert, 0, keepdims=False)
        down_all = lax.dynamic_index_in_dim(w_down, expert, 0, keepdims=False)
        summed = jnp.zeros((rows_in.shape[0], D), jnp.float32)
        for part_index in range(N_EP):
            lower = part_index * slice_width
            upper = lower + slice_width
            gate_pre = jnp.dot(rows_in, gate_all[:, lower:upper], preferred_element_type=jnp.float32)
            up_pre = jnp.dot(rows_in, up_all[:, lower:upper], preferred_element_type=jnp.float32)
            activation = ((up_pre + 1.0) * gate_pre * jax.nn.sigmoid(1.702 * gate_pre)).astype(jnp.bfloat16)
            slice_part = jnp.dot(activation, down_all[:, lower:upper].T, preferred_element_type=jnp.float32).astype(jnp.bfloat16)
            summed = summed + lax.optimization_barrier(slice_part).astype(jnp.float32)
        expert_out = summed.astype(jnp.bfloat16).astype(jnp.float32)
        weight = jnp.where(live, gate_share[safe], jnp.float32(0.0))
        running = running.at[token_at].add(weight[:, None] * expert_out)
        return running, None

    start_acc = jnp.zeros((DOCUMENT_TOKENS, D), jnp.float32)
    total, _ = lax.scan(one_expert, start_acc, jnp.arange(EXPERTS, dtype=jnp.int32))
    return total.astype(jnp.bfloat16)


def reference(hidden, expert_ids, gate_units, w_gate, w_up, w_down):
    return expert_part(hidden, expert_ids, gate_units, w_gate, w_up, w_down)
```

```python
import functools

import jax
import jax.numpy as jnp
from jax import lax
from jax.experimental import pallas as pl
from jax.experimental.pallas import tpu as pltpu
from jax.sharding import PartitionSpec as P

TOP = 4


def slice_output(rows_in, gate_cols, up_cols, down_cols):
    gate_pre = jnp.dot(rows_in, gate_cols, preferred_element_type=jnp.float32)
    up_pre = jnp.dot(rows_in, up_cols, preferred_element_type=jnp.float32)
    activation = ((up_pre + 1.0) * gate_pre * jax.nn.sigmoid(1.702 * gate_pre)).astype(jnp.bfloat16)
    return lax.dot_general(
        activation, down_cols, (((1,), (1,)), ((), ())), preferred_element_type=jnp.float32
    ).astype(jnp.bfloat16)


def routed(hidden, expert_ids, gate_units, w_gate, w_up, w_down):
    token_count, model_width = hidden.shape
    seq_count = lax.axis_size("seq")
    ep_count = lax.axis_size("ep")
    tp_count = lax.axis_size("tp")
    half_width = model_width // tp_count
    my_half = lax.axis_index("tp")
    expert_count = seq_count * tp_count
    capacity = max(2, (token_count * TOP * 11 + expert_count * 8 - 1) // (expert_count * 8))
    flat_ids = expert_ids.reshape(-1)
    onehot_ids = (flat_ids[:, None] == jnp.arange(expert_count, dtype=jnp.int32)[None, :]).astype(
        jnp.int32
    )
    slot_rank = jnp.sum((jnp.cumsum(onehot_ids, axis=0) - 1) * onehot_ids, axis=1)
    owner_seq = flat_ids // tp_count
    owner_half = flat_ids % tp_count
    send_row = jnp.where(owner_half == my_half, owner_seq * capacity + slot_rank, -1)
    selector = jnp.arange(seq_count * capacity, dtype=jnp.int32)[:, None] == send_row[None, :]
    selector = jnp.any(selector.reshape(seq_count * capacity, token_count, TOP), axis=2).astype(
        jnp.bfloat16
    )
    outgoing = jnp.dot(selector, hidden, preferred_element_type=jnp.float32).astype(jnp.bfloat16)
    outgoing = outgoing.reshape(seq_count, capacity, model_width)
    column_of = (owner_half * seq_count + owner_seq) * capacity + slot_rank
    gate_share = gate_units.reshape(-1).astype(jnp.float32) / 65536.0
    column_ids = jnp.arange(tp_count * seq_count * capacity, dtype=jnp.int32)
    combiner = jnp.where(column_ids[None, :] == column_of[:, None], gate_share[:, None], 0.0)
    combiner = jnp.sum(combiner.reshape(token_count, TOP, -1), axis=1)
    copied = jnp.broadcast_to(outgoing[:, None], (seq_count, ep_count, capacity, model_width))
    copied = copied.reshape(seq_count * ep_count, capacity, model_width)
    arrived = lax.all_to_all(copied, ("seq", "ep"), split_axis=0, concat_axis=0, tiled=True)
    slice_rows = slice_output(arrived.reshape(-1, model_width), w_gate[0], w_up[0], w_down[0])
    slice_rows = slice_rows.reshape(seq_count * ep_count, capacity, model_width)
    came_back = lax.all_to_all(
        lax.all_to_all(slice_rows, ("seq", "ep"), split_axis=0, concat_axis=0, tiled=True),
        "tp",
        split_axis=2,
        concat_axis=0,
        tiled=True,
    )
    came_back = came_back.reshape(tp_count, seq_count, ep_count, capacity, half_width)
    returned = jnp.sum(came_back.astype(jnp.float32), axis=2).astype(jnp.bfloat16)
    result_rows = returned.reshape(-1, half_width).astype(jnp.float32)
    moe_out = jnp.dot(
        combiner, result_rows, precision=lax.Precision.HIGHEST, preferred_element_type=jnp.float32
    )
    return moe_out.astype(jnp.bfloat16)


LANES = 128
MESH = pl.DeviceIdType.MESH


def gather_kernel(
    seq_count, hidden_ref, ids_ref, units_ref, gate_hbm, up_hbm, down_hbm, out_ref,
    tokens, gate_w, up_w, down_w, mine, other, other_in, across, across_in, along, along_in,
    load_sem, gz_send, gz_recv, gx_send, gx_recv, gp_send, gp_recv,
    rp_send, rp_recv, rx_send, rx_recv, rz_send, rz_recv,
):
    seq, ep, tp = lax.axis_index("seq"), lax.axis_index("ep"), lax.axis_index("tp")
    rows, width = hidden_ref.shape
    half_rows = rows // 2
    half_width = out_ref.shape[1]
    padded = tokens.shape[2]
    expert_count = seq_count * 2
    side, core = {"ep": 1 - ep}, {"tp": 1 - tp}

    def ahead(step):
        return {"seq": lax.rem(seq + step, seq_count)}

    def behind(step):
        return {"seq": lax.rem(seq + seq_count - step, seq_count)}

    barrier = pltpu.get_barrier_semaphore()
    for peer in [side, core] + [ahead(step) for step in range(1, seq_count)]:
        pl.semaphore_signal(barrier, inc=1, device_id=peer, device_id_type=MESH)

    loads = [
        pltpu.make_async_copy(gate_hbm.at[0], gate_w.at[pl.ds(0, width)], load_sem.at[0]),
        pltpu.make_async_copy(up_hbm.at[0], up_w.at[pl.ds(0, width)], load_sem.at[1]),
        pltpu.make_async_copy(down_hbm.at[0], down_w, load_sem.at[2]),
    ]
    for load in loads:
        load.start()

    tail = width // LANES * LANES
    spare = width - tail
    tokens[0, 0:rows, 0:tail] = hidden_ref[:, 0:tail]
    lane = lax.broadcasted_iota(jnp.int32, (rows, LANES), 1)
    ids, units = ids_ref[...], units_ref[...]
    parts = jnp.zeros((rows, LANES), jnp.int32)
    for choice in range(TOP):
        expert = ids[:, choice : choice + 1]
        unit = units[:, choice : choice + 1]
        parts += jnp.where(lane == expert + spare, unit // 256, 0)
        parts += jnp.where(lane == expert + (spare + expert_count), unit % 256, 0)
    tokens[0, 0:rows, tail:padded] = parts.astype(jnp.float32).astype(jnp.bfloat16)
    tokens[0, 0:rows, tail:width] = hidden_ref[:, tail:width]
    zeros = jnp.zeros((padded - width, gate_w.shape[1]), jnp.bfloat16)
    gate_w[width:padded, :] = zeros
    up_w[width:padded, :] = zeros

    pl.semaphore_wait(barrier, seq_count + 1)

    my_rows = pl.ds(pl.multiple_of(tp * half_rows, half_rows), half_rows)
    my_far_rows = pl.ds(pl.multiple_of(rows + tp * half_rows, half_rows), half_rows)
    sends = []

    def send(src, dst, send_sem, recv_sem, peer):
        copy = pltpu.make_async_remote_copy(
            src_ref=src, dst_ref=dst, send_sem=send_sem, recv_sem=recv_sem,
            device_id=peer, device_id_type=MESH,
        )
        copy.start()
        sends.append(copy)
        return copy

    z_in, x_in, p_in = {}, {}, {}

    def forward_across(step):
        x_in[step] = send(
            tokens.at[step, my_rows], tokens.at[step, my_far_rows],
            gx_send.at[step], gx_recv.at[step], side,
        )

    forward_across(0)
    for step in range(1, seq_count):
        z_in[step] = send(
            tokens.at[0, my_rows], tokens.at[step, my_rows],
            gz_send.at[step], gz_recv.at[step], ahead(step),
        )

    def to_core(step, far):
        where = my_far_rows if far else my_rows
        p_in[step, far] = send(
            tokens.at[step, where], tokens.at[step, where],
            gp_send.at[2 * step + far], gp_recv.at[2 * step + far], core,
        )

    def gather(step):
        if step > 0:
            z_in[step].wait_recv()
            forward_across(step)
            to_core(step, 0)
        x_in[step].wait_recv()
        to_core(step, 1)
        if step > 0:
            p_in[step, 0].wait_recv()
        p_in[step, 1].wait_recv()

    my_expert = seq * 2 + tp
    lanes = lax.broadcasted_iota(jnp.int32, (1, LANES), 1)
    picker = jnp.where(lanes == my_expert + spare, 256.0 / 65536.0, 0.0)
    picker += jnp.where(lanes == my_expert + (spare + expert_count), 1.0 / 65536.0, 0.0)
    r_in, rx_in, rz_in = {}, {}, {}

    def down_part(activation, which):
        cols = down_w[pl.ds(pl.multiple_of(which * half_width, 16), half_width), :]
        return lax.dot_general(
            activation, cols, (((1,), (1,)), ((), ())), preferred_element_type=jnp.float32
        )

    def compute(step):
        rows_in = tokens[step]
        gate_pre = jnp.dot(rows_in, gate_w[...], preferred_element_type=jnp.float32)
        up_pre = jnp.dot(rows_in, up_w[...], preferred_element_type=jnp.float32)
        activation = ((up_pre + 1.0) * gate_pre * jax.nn.sigmoid(1.702 * gate_pre)).astype(jnp.bfloat16)
        share = tokens[step, :, tail:padded].astype(jnp.float32)
        share = jnp.sum(share * picker, axis=1, keepdims=True)
        other[step] = (down_part(activation, 1 - tp) * share).astype(jnp.bfloat16)
        r_in[step] = send(
            other.at[step], other_in.at[step], rp_send.at[step], rp_recv.at[step], core
        )
        mine[step] = down_part(activation, tp) * share

    def join_cores(step):
        r_in[step].wait_recv()
        across[step] = (
            mine[step, rows:, :] + other_in[step, rows:, :].astype(jnp.float32)
        ).astype(jnp.bfloat16)
        rx_in[step] = send(
            across.at[step], across_in.at[step], rx_send.at[step], rx_recv.at[step], side
        )

    def join_sides(step):
        rx_in[step].wait_recv()
        total = mine[step, 0:rows, :] + other_in[step, 0:rows, :].astype(jnp.float32)
        total += across_in[step].astype(jnp.float32)
        if step == 0:
            mine[0, 0:rows, :] = total
        else:
            along[step] = total.astype(jnp.bfloat16)
            rz_in[step] = send(
                along.at[step], along_in.at[step], rz_send.at[step], rz_recv.at[step], behind(step)
            )

    for step in range(seq_count + 2):
        if step < seq_count:
            gather(step)
            if step == 0:
                for load in loads:
                    load.wait()
            compute(step)
        if 1 <= step <= seq_count:
            join_cores(step - 1)
        if step >= 2:
            join_sides(step - 2)

    total = mine[0, 0:rows, :]
    for step in range(1, seq_count):
        rz_in[step].wait_recv()
        total += along_in[step].astype(jnp.float32)
    out_ref[...] = total.astype(jnp.bfloat16)
    for copy in sends:
        copy.wait_send()


def gathered(hidden, expert_ids, gate_units, w_gate, w_up, w_down):
    rows, width = hidden.shape
    units = w_gate.shape[2]
    seq_count = lax.axis_size("seq")
    half = width // 2
    padded = -(-width // LANES) * LANES
    vmem = pl.BlockSpec(memory_space=pltpu.VMEM)
    hbm = pl.BlockSpec(memory_space=pl.ANY)
    dma = pltpu.SemaphoreType.DMA
    sems = [dma((seq_count,))] * 2
    return pl.pallas_call(
        functools.partial(gather_kernel, seq_count),
        out_shape=jax.ShapeDtypeStruct((rows, half), jnp.bfloat16),
        in_specs=[vmem] * 3 + [hbm] * 3,
        out_specs=vmem,
        scratch_shapes=[
            pltpu.VMEM((seq_count, 2 * rows, padded), jnp.bfloat16),
            pltpu.VMEM((padded, units), jnp.bfloat16),
            pltpu.VMEM((padded, units), jnp.bfloat16),
            pltpu.VMEM((width, units), jnp.bfloat16),
            pltpu.VMEM((seq_count, 2 * rows, half), jnp.float32),
            pltpu.VMEM((seq_count, 2 * rows, half), jnp.bfloat16),
            pltpu.VMEM((seq_count, 2 * rows, half), jnp.bfloat16),
            pltpu.VMEM((seq_count, rows, half), jnp.bfloat16),
            pltpu.VMEM((seq_count, rows, half), jnp.bfloat16),
            pltpu.VMEM((seq_count, rows, half), jnp.bfloat16),
            pltpu.VMEM((seq_count, rows, half), jnp.bfloat16),
            dma((3,)),
        ]
        + sems * 2
        + [dma((2 * seq_count,))] * 2
        + sems * 3,
        compiler_params=pltpu.CompilerParams(
            collective_id=0, has_side_effects=True, vmem_limit_bytes=60 * 1024 * 1024
        ),
    )(hidden, expert_ids, gate_units, w_gate, w_up, w_down)


def local(hidden, expert_ids, gate_units, w_gate, w_up, w_down):
    token_count, model_width = hidden.shape
    seq_count = lax.axis_size("seq")
    expert_count = seq_count * lax.axis_size("tp")
    spare = -model_width % LANES
    pairs = lax.axis_size("ep") == 2 and lax.axis_size("tp") == 2
    whole_blocks = 2 * token_count * TOP * 11 >= expert_count * 8 * token_count
    if pairs and whole_blocks and 2 * expert_count <= spare:
        return gathered(hidden, expert_ids, gate_units, w_gate, w_up, w_down)
    return routed(hidden, expert_ids, gate_units, w_gate, w_up, w_down)


def solution(mesh):
    return jax.shard_map(
        local,
        mesh=mesh,
        in_specs=(
            P(("groups", "seq", "ep"), None),
            P(("groups", "seq", "ep"), None),
            P(("groups", "seq", "ep"), None),
            P(("seq", "tp"), None, "ep"),
            P(("seq", "tp"), None, "ep"),
            P(("seq", "tp"), None, "ep"),
        ),
        out_specs=P(("groups", "seq", "ep"), "tp"),
        check_vma=False,
    )
```

```python
import functools

import jax
import jax.numpy as jnp
from jax import lax
from jax.experimental import pallas as pl
from jax.experimental.pallas import tpu as pltpu
from jax.sharding import PartitionSpec as P

TOP = 4


def slice_output(rows_in, gate_cols, up_cols, down_cols):
    gate_pre = jnp.dot(rows_in, gate_cols, preferred_element_type=jnp.float32)
    up_pre = jnp.dot(rows_in, up_cols, preferred_element_type=jnp.float32)
    activation = ((up_pre + 1.0) * gate_pre * jax.nn.sigmoid(1.702 * gate_pre)).astype(jnp.bfloat16)
    return lax.dot_general(
        activation, down_cols, (((1,), (1,)), ((), ())), preferred_element_type=jnp.float32
    ).astype(jnp.bfloat16)


def routed(hidden, expert_ids, gate_units, w_gate, w_up, w_down):
    token_count, model_width = hidden.shape
    seq_count = lax.axis_size("seq")
    ep_count = lax.axis_size("ep")
    tp_count = lax.axis_size("tp")
    half_width = model_width // tp_count
    my_half = lax.axis_index("tp")
    expert_count = seq_count * tp_count
    capacity = max(2, (token_count * TOP * 11 + expert_count * 8 - 1) // (expert_count * 8))
    flat_ids = expert_ids.reshape(-1)
    onehot_ids = (flat_ids[:, None] == jnp.arange(expert_count, dtype=jnp.int32)[None, :]).astype(
        jnp.int32
    )
    slot_rank = jnp.sum((jnp.cumsum(onehot_ids, axis=0) - 1) * onehot_ids, axis=1)
    owner_seq = flat_ids // tp_count
    owner_half = flat_ids % tp_count
    send_row = jnp.where(owner_half == my_half, owner_seq * capacity + slot_rank, -1)
    selector = jnp.arange(seq_count * capacity, dtype=jnp.int32)[:, None] == send_row[None, :]
    selector = jnp.any(selector.reshape(seq_count * capacity, token_count, TOP), axis=2).astype(
        jnp.bfloat16
    )
    outgoing = jnp.dot(selector, hidden, preferred_element_type=jnp.float32).astype(jnp.bfloat16)
    outgoing = outgoing.reshape(seq_count, capacity, model_width)
    column_of = (owner_half * seq_count + owner_seq) * capacity + slot_rank
    gate_share = gate_units.reshape(-1).astype(jnp.float32) / 65536.0
    column_ids = jnp.arange(tp_count * seq_count * capacity, dtype=jnp.int32)
    combiner = jnp.where(column_ids[None, :] == column_of[:, None], gate_share[:, None], 0.0)
    combiner = jnp.sum(combiner.reshape(token_count, TOP, -1), axis=1)
    copied = jnp.broadcast_to(outgoing[:, None], (seq_count, ep_count, capacity, model_width))
    copied = copied.reshape(seq_count * ep_count, capacity, model_width)
    arrived = lax.all_to_all(copied, ("seq", "ep"), split_axis=0, concat_axis=0, tiled=True)
    slice_rows = slice_output(arrived.reshape(-1, model_width), w_gate[0], w_up[0], w_down[0])
    slice_rows = slice_rows.reshape(seq_count * ep_count, capacity, model_width)
    came_back = lax.all_to_all(
        lax.all_to_all(slice_rows, ("seq", "ep"), split_axis=0, concat_axis=0, tiled=True),
        "tp",
        split_axis=2,
        concat_axis=0,
        tiled=True,
    )
    came_back = came_back.reshape(tp_count, seq_count, ep_count, capacity, half_width)
    returned = jnp.sum(came_back.astype(jnp.float32), axis=2).astype(jnp.bfloat16)
    result_rows = returned.reshape(-1, half_width).astype(jnp.float32)
    moe_out = jnp.dot(
        combiner, result_rows, precision=lax.Precision.HIGHEST, preferred_element_type=jnp.float32
    )
    return moe_out.astype(jnp.bfloat16)


LANES = 128
MESH = pl.DeviceIdType.MESH


def gather_kernel(
    seq_count, hidden_ref, ids_ref, units_ref, gate_hbm, up_hbm, down_hbm, out_ref,
    tokens, gate_w, up_w, down_w, mine, other, other_in, across, across_in, along, along_in, final,
    load_sem, gx_send, gx_recv, rp_send, rp_recv, rx_send, rx_recv, rz_send, rz_recv,
    gp_send, gp_recv, gz_send, gz_recv,
):
    seq, ep, tp = lax.axis_index("seq"), lax.axis_index("ep"), lax.axis_index("tp")
    width, rows = hidden_ref.shape
    half_rows = rows // 2
    half_width = out_ref.shape[0]
    padded = tokens.shape[2]
    expert_count = seq_count * 2
    last = seq_count - 1
    side, core = {"ep": 1 - ep}, {"tp": 1 - tp}

    barrier = pltpu.get_barrier_semaphore()
    around = [{"seq": lax.rem(seq + step, seq_count)} for step in range(1, seq_count)]
    for peer in [side, core] + around:
        pl.semaphore_signal(barrier, inc=1, device_id=peer, device_id_type=MESH)

    loads = [
        pltpu.make_async_copy(gate_hbm.at[0], gate_w.at[pl.ds(0, width)], load_sem.at[0]),
        pltpu.make_async_copy(up_hbm.at[0], up_w.at[pl.ds(0, width)], load_sem.at[1]),
        pltpu.make_async_copy(down_hbm.at[0], down_w, load_sem.at[2]),
    ]
    for load in loads:
        load.start()

    tail = width // LANES * LANES
    first = width - tail
    slot = lax.broadcasted_iota(jnp.int32, (LANES, rows), 0)
    parts = jnp.zeros((LANES, rows), jnp.int32)
    for choice in range(TOP):
        expert = ids_ref[choice : choice + 1, :]
        unit = units_ref[choice : choice + 1, :]
        parts += jnp.where(slot == expert + first, unit // 256, 0)
        parts += jnp.where(slot == expert + (first + expert_count), unit % 256, 0)
    parts = parts.astype(jnp.float32)
    if first:
        rest = hidden_ref[tail:width, :].astype(jnp.float32)
        parts += jnp.concatenate([rest, jnp.zeros((LANES - first, rows), jnp.float32)], axis=0)
    tokens[seq, 0:rows, tail:padded] = parts.T.astype(jnp.bfloat16)
    for low in range(0, tail, LANES):
        piece = hidden_ref[low : low + LANES, :].astype(jnp.float32)
        tokens[seq, 0:rows, low : low + LANES] = piece.T.astype(jnp.bfloat16)
    zeros = jnp.zeros((padded - width, gate_w.shape[1]), jnp.bfloat16)
    gate_w[width:padded, :] = zeros
    up_w[width:padded, :] = zeros

    pl.semaphore_wait(barrier, seq_count + 1)

    my_rows = pl.ds(pl.multiple_of(tp * half_rows, half_rows), half_rows)
    my_far_rows = pl.ds(pl.multiple_of(rows + tp * half_rows, half_rows), half_rows)
    sends = []

    def describe(src, dst, send_sem, recv_sem, peer):
        return pltpu.make_async_remote_copy(
            src_ref=src, dst_ref=dst, send_sem=send_sem, recv_sem=recv_sem,
            device_id=peer, device_id_type=MESH,
        )

    def send(*parts, when=None):
        if when is None:
            copy = describe(*parts)
            copy.start()
            sends.append((copy, None, None))
            return copy

        @pl.when(when)
        def _():
            describe(*parts).start()

        sends.append((None, parts, when))

    short = jnp.minimum(seq, last - seq)
    blocks, signs = [seq], [None]
    for event in range(1, seq_count):
        paired = event <= 2 * short
        sign = jnp.where(paired, 1 - 2 * (event % 2), jnp.where(seq < last - seq, 1, -1))
        distance = jnp.where(paired, (event + 1) // 2, event - short)
        blocks.append(seq + sign * distance)
        signs.append(sign)

    x_in, p_in, r_in, rx_in = {}, {}, {}, {}

    def block_along(event, sem, onward, when):
        block = blocks[event]
        where = tokens.at[block, my_rows]
        send(where, where, gz_send.at[sem], gz_recv.at[block], {"seq": onward}, when=when)

    def block_across(event):
        block = blocks[event]
        x_in[event] = send(
            tokens.at[block, my_rows], tokens.at[block, my_far_rows],
            gx_send.at[event], gx_recv.at[event], side,
        )

    def to_core(event, far):
        where = tokens.at[blocks[event], my_far_rows if far else my_rows]
        p_in[event, far] = send(
            where, where, gp_send.at[2 * event + far], gp_recv.at[2 * event + far], core
        )

    def arrive(event):
        block = blocks[event]
        where = tokens.at[block, my_rows]
        describe(where, where, gz_send.at[event], gz_recv.at[block], side).wait_recv()
        onward = seq - signs[event]
        inside = jnp.logical_and(onward >= 0, onward <= last)
        block_along(event, event, jnp.clip(onward, 0, last), inside)
        block_across(event)
        to_core(event, 0)

    my_expert = seq * 2 + tp
    lanes = lax.broadcasted_iota(jnp.int32, (1, LANES), 1)
    picker = jnp.where(lanes == my_expert + first, 256.0 / 65536.0, 0.0)
    picker += jnp.where(lanes == my_expert + (first + expert_count), 1.0 / 65536.0, 0.0)

    def down_part(activation, which):
        cols = down_w[pl.ds(pl.multiple_of(which * half_width, 16), half_width), :]
        return lax.dot_general(
            activation, cols, (((1,), (1,)), ((), ())), preferred_element_type=jnp.float32
        )

    def compute(event):
        x_in[event].wait_recv()
        to_core(event, 1)
        if event > 0:
            p_in[event, 0].wait_recv()
        p_in[event, 1].wait_recv()
        block = blocks[event]
        rows_in = tokens[block]
        gate_pre = jnp.dot(rows_in, gate_w[...], preferred_element_type=jnp.float32)
        up_pre = jnp.dot(rows_in, up_w[...], preferred_element_type=jnp.float32)
        activation = ((up_pre + 1.0) * gate_pre * jax.nn.sigmoid(1.702 * gate_pre)).astype(jnp.bfloat16)
        share = tokens[block, :, tail:padded].astype(jnp.float32)
        share = jnp.sum(share * picker, axis=1, keepdims=True)
        other[event] = (down_part(activation, 1 - tp) * share).astype(jnp.bfloat16)
        r_in[event] = send(
            other.at[event], other_in.at[event], rp_send.at[event], rp_recv.at[event], core
        )
        mine[event] = down_part(activation, tp) * share

    def join_cores(event):
        r_in[event].wait_recv()
        across[event] = (
            mine[event, rows:, :] + other_in[event, rows:, :].astype(jnp.float32)
        ).astype(jnp.bfloat16)
        rx_in[event] = send(
            across.at[event], across_in.at[event], rx_send.at[event], rx_recv.at[event], side
        )

    def join_sides(event):
        rx_in[event].wait_recv()
        total = mine[event, 0:rows, :] + other_in[event, 0:rows, :].astype(jnp.float32)
        total += across_in[event].astype(jnp.float32)
        if event == 0:
            return total
        along[event] = total.astype(jnp.bfloat16)
        send(
            along.at[event], along_in.at[seq], rz_send.at[event], rz_recv.at[seq],
            {"seq": blocks[event]},
        )

    block_across(0)
    block_along(0, 0, jnp.minimum(seq + 1, last), seq < last)
    block_along(0, seq_count, jnp.maximum(seq - 1, 0), seq > 0)
    for event in range(1, min(3, seq_count)):
        arrive(event)
    for load in loads:
        load.wait()
    compute(0)
    for event in range(1, seq_count):
        if event + 2 < seq_count:
            arrive(event + 2)
        compute(event)
        join_cores(event)
        if event > 1:
            join_sides(event - 1)
    join_cores(0)
    if last > 0:
        join_sides(last)
    total = join_sides(0)
    for event in range(1, seq_count):
        source = blocks[event]
        describe(
            along.at[event], along_in.at[source], rz_send.at[event], rz_recv.at[source], side
        ).wait_recv()
        total += along_in[source].astype(jnp.float32)
    final[:, 0:half_width] = total
    for low in range(0, half_width, LANES):
        count = min(LANES, half_width - low)
        piece = final[:, low : low + LANES].T
        out_ref[low : low + count, :] = piece[0:count, :].astype(jnp.bfloat16)
    for copy, parts, when in sends:
        if when is None:
            copy.wait_send()
        else:
            pl.when(when)(lambda parts=parts: describe(*parts).wait_send())


def gathered(hidden, expert_ids, gate_units, w_gate, w_up, w_down):
    rows, width = hidden.shape
    units = w_gate.shape[2]
    seq_count = lax.axis_size("seq")
    half = width // 2
    padded = -(-width // LANES) * LANES
    vmem = pl.BlockSpec(memory_space=pltpu.VMEM)
    hbm = pl.BlockSpec(memory_space=pl.ANY)
    dma = pltpu.SemaphoreType.DMA
    sems = [dma((seq_count,))] * 2
    return pl.pallas_call(
        functools.partial(gather_kernel, seq_count),
        out_shape=jax.ShapeDtypeStruct((half, rows), jnp.bfloat16),
        in_specs=[vmem] * 3 + [hbm] * 3,
        out_specs=vmem,
        scratch_shapes=[
            pltpu.VMEM((seq_count, 2 * rows, padded), jnp.bfloat16),
            pltpu.VMEM((padded, units), jnp.bfloat16),
            pltpu.VMEM((padded, units), jnp.bfloat16),
            pltpu.VMEM((width, units), jnp.bfloat16),
            pltpu.VMEM((seq_count, 2 * rows, half), jnp.float32),
            pltpu.VMEM((seq_count, 2 * rows, half), jnp.bfloat16),
            pltpu.VMEM((seq_count, 2 * rows, half), jnp.bfloat16),
            pltpu.VMEM((seq_count, rows, half), jnp.bfloat16),
            pltpu.VMEM((seq_count, rows, half), jnp.bfloat16),
            pltpu.VMEM((seq_count, rows, half), jnp.bfloat16),
            pltpu.VMEM((seq_count, rows, half), jnp.bfloat16),
            pltpu.VMEM((rows, -(-half // LANES) * LANES), jnp.float32),
            dma((3,)),
        ]
        + sems * 4
        + [dma((2 * seq_count,))] * 2
        + [dma((seq_count + 1,)), dma((seq_count,))],
        compiler_params=pltpu.CompilerParams(
            collective_id=0, has_side_effects=True, vmem_limit_bytes=60 * 1024 * 1024
        ),
    )(hidden.T, expert_ids.T, gate_units.T, w_gate, w_up, w_down).T


def local(hidden, expert_ids, gate_units, w_gate, w_up, w_down):
    token_count, model_width = hidden.shape
    seq_count = lax.axis_size("seq")
    expert_count = seq_count * lax.axis_size("tp")
    spare = -model_width % LANES
    pairs = lax.axis_size("ep") == 2 and lax.axis_size("tp") == 2
    whole_blocks = 2 * token_count * TOP * 11 >= expert_count * 8 * token_count
    if pairs and whole_blocks and 2 * expert_count <= spare:
        return gathered(hidden, expert_ids, gate_units, w_gate, w_up, w_down)
    return routed(hidden, expert_ids, gate_units, w_gate, w_up, w_down)


def solution(mesh):
    return jax.shard_map(
        local,
        mesh=mesh,
        in_specs=(
            P(("groups", "seq", "ep"), None),
            P(("groups", "seq", "ep"), None),
            P(("groups", "seq", "ep"), None),
            P(("seq", "tp"), None, "ep"),
            P(("seq", "tp"), None, "ep"),
            P(("seq", "tp"), None, "ep"),
        ),
        out_specs=P(("groups", "seq", "ep"), "tp"),
        check_vma=False,
    )
```

```python
import functools

import jax
import jax.numpy as jnp
from jax import lax
from jax.experimental import pallas as pl
from jax.experimental.pallas import tpu as pltpu
from jax.sharding import PartitionSpec as P

TOP = 4


def slice_output(rows_in, gate_cols, up_cols, down_cols):
    gate_pre = jnp.dot(rows_in, gate_cols, preferred_element_type=jnp.float32)
    up_pre = jnp.dot(rows_in, up_cols, preferred_element_type=jnp.float32)
    activation = ((up_pre + 1.0) * gate_pre * jax.nn.sigmoid(1.702 * gate_pre)).astype(jnp.bfloat16)
    return lax.dot_general(
        activation, down_cols, (((1,), (1,)), ((), ())), preferred_element_type=jnp.float32
    ).astype(jnp.bfloat16)


def routed(hidden, expert_ids, gate_units, w_gate, w_up, w_down):
    token_count, model_width = hidden.shape
    seq_count = lax.axis_size("seq")
    ep_count = lax.axis_size("ep")
    tp_count = lax.axis_size("tp")
    half_width = model_width // tp_count
    my_half = lax.axis_index("tp")
    expert_count = seq_count * tp_count
    capacity = max(2, (token_count * TOP * 11 + expert_count * 8 - 1) // (expert_count * 8))
    flat_ids = expert_ids.reshape(-1)
    onehot_ids = (flat_ids[:, None] == jnp.arange(expert_count, dtype=jnp.int32)[None, :]).astype(
        jnp.int32
    )
    slot_rank = jnp.sum((jnp.cumsum(onehot_ids, axis=0) - 1) * onehot_ids, axis=1)
    owner_seq = flat_ids // tp_count
    owner_half = flat_ids % tp_count
    send_row = jnp.where(owner_half == my_half, owner_seq * capacity + slot_rank, -1)
    selector = jnp.arange(seq_count * capacity, dtype=jnp.int32)[:, None] == send_row[None, :]
    selector = jnp.any(selector.reshape(seq_count * capacity, token_count, TOP), axis=2).astype(
        jnp.bfloat16
    )
    outgoing = jnp.dot(selector, hidden, preferred_element_type=jnp.float32).astype(jnp.bfloat16)
    outgoing = outgoing.reshape(seq_count, capacity, model_width)
    column_of = (owner_half * seq_count + owner_seq) * capacity + slot_rank
    gate_share = gate_units.reshape(-1).astype(jnp.float32) / 65536.0
    column_ids = jnp.arange(tp_count * seq_count * capacity, dtype=jnp.int32)
    combiner = jnp.where(column_ids[None, :] == column_of[:, None], gate_share[:, None], 0.0)
    combiner = jnp.sum(combiner.reshape(token_count, TOP, -1), axis=1)
    copied = jnp.broadcast_to(outgoing[:, None], (seq_count, ep_count, capacity, model_width))
    copied = copied.reshape(seq_count * ep_count, capacity, model_width)
    arrived = lax.all_to_all(copied, ("seq", "ep"), split_axis=0, concat_axis=0, tiled=True)
    slice_rows = slice_output(arrived.reshape(-1, model_width), w_gate[0], w_up[0], w_down[0])
    slice_rows = slice_rows.reshape(seq_count * ep_count, capacity, model_width)
    came_back = lax.all_to_all(
        lax.all_to_all(slice_rows, ("seq", "ep"), split_axis=0, concat_axis=0, tiled=True),
        "tp",
        split_axis=2,
        concat_axis=0,
        tiled=True,
    )
    came_back = came_back.reshape(tp_count, seq_count, ep_count, capacity, half_width)
    returned = jnp.sum(came_back.astype(jnp.float32), axis=2).astype(jnp.bfloat16)
    result_rows = returned.reshape(-1, half_width).astype(jnp.float32)
    moe_out = jnp.dot(
        combiner, result_rows, precision=lax.Precision.HIGHEST, preferred_element_type=jnp.float32
    )
    return moe_out.astype(jnp.bfloat16)


LANES = 128
MESH = pl.DeviceIdType.MESH


def gather_kernel(
    seq_count, hidden_ref, ids_ref, units_ref, gate_hbm, up_hbm, down_hbm, out_ref,
    tokens, gate_w, up_w, down_w, mine, other, other_in, across, across_in, along, along_in,
    load_sem, gx_send, gx_recv, rp_send, rp_recv, rx_send, rx_recv, rz_send, rz_recv,
    gp_send, gp_recv, gz_send, gz_recv,
):
    seq, ep, tp = lax.axis_index("seq"), lax.axis_index("ep"), lax.axis_index("tp")
    width, rows = hidden_ref.shape
    half_rows = rows // 2
    half_width = out_ref.shape[0]
    padded = tokens.shape[2]
    expert_count = seq_count * 2
    last = seq_count - 1
    side, core = {"ep": 1 - ep}, {"tp": 1 - tp}

    barrier = pltpu.get_barrier_semaphore()
    around = [{"seq": lax.rem(seq + step, seq_count)} for step in range(1, seq_count)]
    for peer in [side, core] + around:
        pl.semaphore_signal(barrier, inc=1, device_id=peer, device_id_type=MESH)

    loads = [
        pltpu.make_async_copy(gate_hbm.at[0], gate_w.at[pl.ds(0, width)], load_sem.at[0]),
        pltpu.make_async_copy(up_hbm.at[0], up_w.at[pl.ds(0, width)], load_sem.at[1]),
        pltpu.make_async_copy(down_hbm.at[0], down_w, load_sem.at[2]),
    ]
    for load in loads:
        load.start()

    tail = width // LANES * LANES
    first = width - tail
    slot = lax.broadcasted_iota(jnp.int32, (LANES, rows), 0)
    parts = jnp.zeros((LANES, rows), jnp.int32)
    for choice in range(TOP):
        expert = ids_ref[choice : choice + 1, :]
        unit = units_ref[choice : choice + 1, :]
        parts += jnp.where(slot == expert + first, unit // 256, 0)
        parts += jnp.where(slot == expert + (first + expert_count), unit % 256, 0)
    parts = parts.astype(jnp.float32)
    if first:
        rest = hidden_ref[tail:width, :].astype(jnp.float32)
        parts += jnp.concatenate([rest, jnp.zeros((LANES - first, rows), jnp.float32)], axis=0)
    tokens[seq, 0:rows, tail:padded] = parts.T.astype(jnp.bfloat16)
    for low in range(0, tail, LANES):
        piece = hidden_ref[low : low + LANES, :].astype(jnp.float32)
        tokens[seq, 0:rows, low : low + LANES] = piece.T.astype(jnp.bfloat16)
    zeros = jnp.zeros((padded - width, gate_w.shape[1]), jnp.bfloat16)
    gate_w[width:padded, :] = zeros
    up_w[width:padded, :] = zeros

    pl.semaphore_wait(barrier, seq_count + 1)

    my_rows = pl.ds(pl.multiple_of(tp * half_rows, half_rows), half_rows)
    my_far_rows = pl.ds(pl.multiple_of(rows + tp * half_rows, half_rows), half_rows)
    sends = []

    def describe(src, dst, send_sem, recv_sem, peer):
        return pltpu.make_async_remote_copy(
            src_ref=src, dst_ref=dst, send_sem=send_sem, recv_sem=recv_sem,
            device_id=peer, device_id_type=MESH,
        )

    def send(*parts, when=None):
        if when is None:
            copy = describe(*parts)
            copy.start()
            sends.append((copy, None, None))
            return copy

        @pl.when(when)
        def _():
            describe(*parts).start()

        sends.append((None, parts, when))

    short = jnp.minimum(seq, last - seq)
    blocks, signs = [seq], [None]
    for event in range(1, seq_count):
        paired = event <= 2 * short
        sign = jnp.where(paired, 1 - 2 * (event % 2), jnp.where(seq < last - seq, 1, -1))
        distance = jnp.where(paired, (event + 1) // 2, event - short)
        blocks.append(seq + sign * distance)
        signs.append(sign)

    x_in, p_in, r_in, rx_in = {}, {}, {}, {}

    def block_along(event, sem, onward, when):
        block = blocks[event]
        where = tokens.at[block, my_rows]
        send(where, where, gz_send.at[sem], gz_recv.at[block], {"seq": onward}, when=when)

    def block_across(event):
        block = blocks[event]
        x_in[event] = send(
            tokens.at[block, my_rows], tokens.at[block, my_far_rows],
            gx_send.at[event], gx_recv.at[event], side,
        )

    def to_core(event, far):
        where = tokens.at[blocks[event], my_far_rows if far else my_rows]
        p_in[event, far] = send(
            where, where, gp_send.at[2 * event + far], gp_recv.at[2 * event + far], core
        )

    def arrive(event):
        block = blocks[event]
        where = tokens.at[block, my_rows]
        describe(where, where, gz_send.at[event], gz_recv.at[block], side).wait_recv()
        onward = seq - signs[event]
        inside = jnp.logical_and(onward >= 0, onward <= last)
        block_along(event, event, jnp.clip(onward, 0, last), inside)
        block_across(event)
        to_core(event, 0)

    my_expert = seq * 2 + tp
    lanes = lax.broadcasted_iota(jnp.int32, (LANES, 1), 0)
    picker = jnp.where(lanes == my_expert + first, 256.0 / 65536.0, 0.0)
    picker += jnp.where(lanes == my_expert + (first + expert_count), 1.0 / 65536.0, 0.0)

    def down_part(activation, which):
        cols = down_w[pl.ds(pl.multiple_of(which * half_width, 16), half_width), :]
        return lax.dot_general(
            cols, activation, (((1,), (1,)), ((), ())), preferred_element_type=jnp.float32
        )

    def compute(event):
        x_in[event].wait_recv()
        to_core(event, 1)
        if event > 0:
            p_in[event, 0].wait_recv()
        p_in[event, 1].wait_recv()
        block = blocks[event]
        rows_in = tokens[block]
        gate_pre = jnp.dot(rows_in, gate_w[...], preferred_element_type=jnp.float32)
        up_pre = jnp.dot(rows_in, up_w[...], preferred_element_type=jnp.float32)
        activation = ((up_pre + 1.0) * gate_pre * jax.nn.sigmoid(1.702 * gate_pre)).astype(jnp.bfloat16)
        share = tokens[block, :, tail:padded].astype(jnp.float32).T
        share = jnp.sum(share * picker, axis=0, keepdims=True)
        other[event] = (down_part(activation, 1 - tp) * share).astype(jnp.bfloat16)
        r_in[event] = send(
            other.at[event], other_in.at[event], rp_send.at[event], rp_recv.at[event], core
        )
        mine[event] = down_part(activation, tp) * share

    def join_cores(event):
        r_in[event].wait_recv()
        across[event] = (
            mine[event, :, rows:] + other_in[event, :, rows:].astype(jnp.float32)
        ).astype(jnp.bfloat16)
        rx_in[event] = send(
            across.at[event], across_in.at[event], rx_send.at[event], rx_recv.at[event], side
        )

    def join_sides(event):
        rx_in[event].wait_recv()
        total = mine[event, :, 0:rows] + other_in[event, :, 0:rows].astype(jnp.float32)
        total += across_in[event].astype(jnp.float32)
        if event == 0:
            return total
        along[event] = total.astype(jnp.bfloat16)
        send(
            along.at[event], along_in.at[seq], rz_send.at[event], rz_recv.at[seq],
            {"seq": blocks[event]},
        )

    block_across(0)
    block_along(0, 0, jnp.minimum(seq + 1, last), seq < last)
    block_along(0, seq_count, jnp.maximum(seq - 1, 0), seq > 0)
    for event in range(1, min(3, seq_count)):
        arrive(event)
    for load in loads:
        load.wait()
    compute(0)
    for event in range(1, seq_count):
        if event + 2 < seq_count:
            arrive(event + 2)
        compute(event)
        join_cores(event)
        if event > 1:
            join_sides(event - 1)
    join_cores(0)
    if last > 0:
        join_sides(last)
    total = join_sides(0)
    for event in range(1, seq_count):
        source = blocks[event]
        describe(
            along.at[event], along_in.at[source], rz_send.at[event], rz_recv.at[source], side
        ).wait_recv()
        total += along_in[source].astype(jnp.float32)
    out_ref[...] = total.astype(jnp.bfloat16)
    for copy, parts, when in sends:
        if when is None:
            copy.wait_send()
        else:
            pl.when(when)(lambda parts=parts: describe(*parts).wait_send())


def gathered(hidden, expert_ids, gate_units, w_gate, w_up, w_down):
    rows, width = hidden.shape
    units = w_gate.shape[2]
    seq_count = lax.axis_size("seq")
    half = width // 2
    padded = -(-width // LANES) * LANES
    vmem = pl.BlockSpec(memory_space=pltpu.VMEM)
    hbm = pl.BlockSpec(memory_space=pl.ANY)
    dma = pltpu.SemaphoreType.DMA
    sems = [dma((seq_count,))] * 2
    return pl.pallas_call(
        functools.partial(gather_kernel, seq_count),
        out_shape=jax.ShapeDtypeStruct((half, rows), jnp.bfloat16),
        in_specs=[vmem] * 3 + [hbm] * 3,
        out_specs=vmem,
        scratch_shapes=[
            pltpu.VMEM((seq_count, 2 * rows, padded), jnp.bfloat16),
            pltpu.VMEM((padded, units), jnp.bfloat16),
            pltpu.VMEM((padded, units), jnp.bfloat16),
            pltpu.VMEM((width, units), jnp.bfloat16),
            pltpu.VMEM((seq_count, half, 2 * rows), jnp.float32),
            pltpu.VMEM((seq_count, half, 2 * rows), jnp.bfloat16),
            pltpu.VMEM((seq_count, half, 2 * rows), jnp.bfloat16),
            pltpu.VMEM((seq_count, half, rows), jnp.bfloat16),
            pltpu.VMEM((seq_count, half, rows), jnp.bfloat16),
            pltpu.VMEM((seq_count, half, rows), jnp.bfloat16),
            pltpu.VMEM((seq_count, half, rows), jnp.bfloat16),
            dma((3,)),
        ]
        + sems * 4
        + [dma((2 * seq_count,))] * 2
        + [dma((seq_count + 1,)), dma((seq_count,))],
        compiler_params=pltpu.CompilerParams(
            collective_id=0, has_side_effects=True, vmem_limit_bytes=60 * 1024 * 1024
        ),
    )(hidden.T, expert_ids.T, gate_units.T, w_gate, w_up, w_down).T


def local(hidden, expert_ids, gate_units, w_gate, w_up, w_down):
    token_count, model_width = hidden.shape
    seq_count = lax.axis_size("seq")
    expert_count = seq_count * lax.axis_size("tp")
    spare = -model_width % LANES
    pairs = lax.axis_size("ep") == 2 and lax.axis_size("tp") == 2
    whole_blocks = 2 * token_count * TOP * 11 >= expert_count * 8 * token_count
    if pairs and whole_blocks and 2 * expert_count <= spare:
        return gathered(hidden, expert_ids, gate_units, w_gate, w_up, w_down)
    return routed(hidden, expert_ids, gate_units, w_gate, w_up, w_down)


def solution(mesh):
    return jax.shard_map(
        local,
        mesh=mesh,
        in_specs=(
            P(("groups", "seq", "ep"), None),
            P(("groups", "seq", "ep"), None),
            P(("groups", "seq", "ep"), None),
            P(("seq", "tp"), None, "ep"),
            P(("seq", "tp"), None, "ep"),
            P(("seq", "tp"), None, "ep"),
        ),
        out_specs=P(("groups", "seq", "ep"), "tp"),
        check_vma=False,
    )
```
